32 devices in a mesh: dp: 16 (over z, y, core), tensor: 2 (over x).
Axes of the slice: x: 2, y: 2, z: 4, core: 2. Of those that a mesh axis runs over, the one named last changes fastest.
Arguments:
- tokens: bfloat16 [32768, 768], P(('dp', 'tensor')), may hold values from -6 to 6
- w_qkv: bfloat16 [3, 768, 768], P(None, None, 'tensor'), may hold values from -0.21875 to 0.21875
- bias_qv: bfloat16 [2, 768], P(None, 'tensor'), may hold values from -3 to 3
- w_out: bfloat16 [768, 768], P('tensor'), may hold values from -0.625 to 0.625
- bias_out: bfloat16 [768], replicated, may hold values from -3 to 3
- gain_attn: bfloat16 [768], replicated, may hold values from 0.099609375 to 1.8984375
- shift_attn: bfloat16 [768], replicated, may hold values from -3 to 3
- w_up: bfloat16 [768, 3072], P(None, 'tensor'), may hold values from -0.21875 to 0.21875
- bias_up: bfloat16 [3072], P('tensor'), may hold values from -3 to 3
- w_down: bfloat16 [3072, 768], P('tensor'), may hold values from -0.15625 to 0.15625
- bias_down: bfloat16 [768], replicated, may hold values from -3 to 3
- gain_ffn: bfloat16 [768], replicated, may hold values from 0.099609375 to 1.8984375
- shift_ffn: bfloat16 [768], replicated, may hold values from -3 to 3
- cotangent: bfloat16 [32768, 768], P(('dp', 'tensor')), may hold values from -6 to 6
- span_start: int32 [64, 26], P('dp'), may hold values from 0 to 509
- span_len: int32 [64, 26], P('dp'), may hold values from 1 to 3
Outputs:
- layer_output: bfloat16 [32768, 768], P(('dp', 'tensor'))
- grad_tokens: bfloat16 [32768, 768], P(('dp', 'tensor'))
- grad_qkv: float32 [3, 768, 768], P(None, None, 'tensor')
- grad_bias_qv: float32 [2, 768], P(None, 'tensor')
- grad_out: float32 [768, 768], P('tensor')
- grad_bias_out: float32 [768], replicated
- grad_gain_attn: float32 [768], replicated
- grad_shift_attn: float32 [768], replicated
- grad_up: float32 [768, 3072], P(None, 'tensor')
- grad_bias_up: float32 [3072], P('tensor')
- grad_down: float32 [3072, 768], P('tensor')
- grad_bias_down: float32 [768], replicated
- grad_gain_ffn: float32 [768], replicated
- grad_shift_ffn: float32 [768], replicated
The draws below stay inside these ranges and needn't reach their ends.
Inputs may be any that keep to these rules, and one draw needn't show every extreme that they name: `span_start`: span starts leave room for a span of 3.
All inputs are finite; a program needn't handle non-finite values.
Results may differ from the reference program's by a relative error of at most 0.014.
The reference program's roundings to bfloat16 on the way count: a program that leaves them out, or rounds other values in their place, can miss the bound.
Values may be sent and summed in bfloat16 or wider, within the bound.
No kernel may reach another device: no remote copies, remote signals or barrier semaphores. Data moves between devices by JAX's collectives and lax.ppermute only.
A program may use at most 128 MiB of HBM per device.

```python
import math
import jax
import jax.numpy as jnp
from jax import lax

D = 768
HEADS = 12
FF = 3072
HEAD = 64
SEQ = 512
SPANS = 26
SEQS = 64
TOKENS = 32768


def set_ends(result, own_key, low, top_value):
    place = [jax.random.randint(jax.random.fold_in(own_key, axis), (), 0, length) for axis, length in enumerate(result.shape)]
    longest = result.shape.index(max(result.shape))
    neighbour = place[:longest] + [(place[longest] + 1) % result.shape[longest]] + place[longest + 1:]
    return result.at[tuple(place)].set(low).at[tuple(neighbour)].set(top_value)


def block_scale(stream_key, extent, split, least, top_value):
    factor_of = 1.0
    for position, parts in split:
        draws = jax.random.uniform(jax.random.fold_in(jax.random.fold_in(stream_key, 6), position), (parts,), jnp.float32, least / len(split), top_value / len(split))
        factor_of = factor_of * jnp.repeat(jnp.exp(draws), extent[position] // parts).reshape((-1,) + (1,) * (len(extent) - 1 - position))
    return factor_of


def gaussian(key, dims, spread, most, shards=(), held_as=jnp.bfloat16):
    values = spread * jax.random.normal(key, dims, jnp.float32)
    if shards:
        values = values * block_scale(key, dims, shards, -0.22, 0.18)
    return jnp.clip(values, -most, most).astype(held_as)


def setup_inputs(seed: int = 0) -> dict:
    splits = jax.random.split(jax.random.key(seed), 17)
    tokens = gaussian(splits[0], (TOKENS, D), 1.0, 6.0, ((0, 32),))
    w_qkv = gaussian(splits[1], (3, D, D), D ** -0.5, 0.21875, ((2, 2),))
    bias_qv = gaussian(splits[2], (2, D), 0.5, 3.0, ((1, 2),))
    w_out = gaussian(splits[3], (D, D), (D // 8) ** -0.5, 0.625, ((0, 2),))
    bias_out = gaussian(splits[4], (D,), 0.5, 3.0)
    gain_attn = jnp.clip(1.0 + 0.18 * jax.random.normal(splits[5], (D,), jnp.float32), 0.099609375, 1.8984375).astype(jnp.bfloat16)
    shift_attn = gaussian(splits[6], (D,), 0.5, 3.0)
    w_up = gaussian(splits[7], (D, FF), D ** -0.5, 0.21875, ((1, 2),))
    bias_up = gaussian(splits[8], (FF,), 0.5, 3.0, ((0, 2),))
    w_down = gaussian(splits[9], (FF, D), (FF // 2) ** -0.5, 0.15625, ((0, 2),))
    bias_down = gaussian(splits[10], (D,), 0.5, 3.0)
    gain_ffn = jnp.clip(1.0 + 0.18 * jax.random.normal(splits[11], (D,), jnp.float32), 0.099609375, 1.8984375).astype(jnp.bfloat16)
    shift_ffn = gaussian(splits[12], (D,), 0.5, 3.0)
    cotangent = gaussian(splits[13], (TOKENS, D), 1.0, 6.0, ((0, 32),))
    span_start = set_ends(jax.random.randint(splits[14], (SEQS, SPANS), 0, SEQ - 2), jax.random.fold_in(splits[14], 1), 0, (SEQ - 2) - 1).astype(jnp.int32)
    span_len = set_ends(jax.random.randint(splits[15], (SEQS, SPANS), 1, 4), jax.random.fold_in(splits[15], 1), 1, 3).astype(jnp.int32)
    return dict(tokens=tokens, w_qkv=w_qkv, bias_qv=bias_qv, w_out=w_out, bias_out=bias_out, gain_attn=gain_attn, shift_attn=shift_attn, w_up=w_up, bias_up=bias_up, w_down=w_down, bias_down=bias_down, gain_ffn=gain_ffn, shift_ffn=shift_ffn, cotangent=cotangent, span_start=span_start, span_len=span_len)


HIGHEST = lax.Precision.HIGHEST
NORM_EPSILON = 1e-12

@jax.custom_vjp
def low(v):
    return lax.optimization_barrier(v.astype(jnp.bfloat16)).astype(jnp.float32)

@jax.custom_vjp
def low_back(v):
    return v

def low_keep(v):
    return (low(v), None)

def low_pass(kept, grad):
    return (grad,)

def back_keep(v):
    return (v, None)

def back_low(kept, grad):
    return (low(grad),)
low.defvjp(low_keep, low_pass)
low_back.defvjp(back_keep, back_low)

def gelu_tanh(values):
    return jax.nn.gelu(values, approximate=True)

def layer_norm(values, gain_vec, shift_vec):
    row_mean = lax.optimization_barrier(jnp.mean(values, -1, keepdims=True))
    centered = values - row_mean
    variance = lax.optimization_barrier(jnp.mean(centered * centered, -1, keepdims=True))
    return centered * lax.rsqrt(variance + NORM_EPSILON) * gain_vec + shift_vec

def attend_one(pieces):
    queries, keys, values = pieces
    scores = jnp.einsum('qhd,khd->hqk', queries, keys, precision=HIGHEST) * HEAD ** (-0.5)
    probs = low(jax.nn.softmax(low_back(scores), axis=-1))
    return jnp.einsum('hqk,khd->qhd', probs, values, precision=HIGHEST)

def forward(x_rows, params):
    w_qkv, bias_qv, w_out, bias_out, gain_attn, shift_attn, w_up, bias_up, w_down, bias_down, gain_ffn, shift_ffn = params
    bias_three = jnp.stack([bias_qv[0], jnp.zeros_like(bias_qv[0]), bias_qv[1]])
    qkv = jnp.einsum('td,cde->cte', x_rows, w_qkv, precision=HIGHEST) + bias_three[:, None, :]
    qkv = low_back(low(qkv))
    head_view = qkv.reshape(3, -1, SEQ, HEADS, HEAD)
    context = lax.map(jax.checkpoint(attend_one), (head_view[0], head_view[1], head_view[2]))
    context = low_back(low(context.reshape(-1, D)))
    attention = low_back(jnp.dot(context, w_out, precision=HIGHEST) + bias_out)
    hidden = layer_norm(x_rows + attention, gain_attn, shift_attn)
    pre_gelu = low_back(jnp.dot(low(hidden), w_up, precision=HIGHEST) + bias_up)
    activated = low(gelu_tanh(pre_gelu))
    ffn_out = low_back(jnp.dot(activated, w_down, precision=HIGHEST) + bias_down)
    return layer_norm(hidden + ffn_out, gain_ffn, shift_ffn)

def span_mask(starts, lengths_in):
    positions = jnp.arange(SEQ, dtype=jnp.int32)
    inside = (positions[None, None, :] >= starts[:, :, None]) & (positions[None, None, :] < (starts + lengths_in)[:, :, None])
    return jnp.any(inside, axis=1).astype(jnp.float32).reshape(-1)

def reference(tokens, w_qkv, bias_qv, w_out, bias_out, gain_attn, shift_attn, w_up, bias_up, w_down, bias_down, gain_ffn, shift_ffn, cotangent, span_start, span_len):
    params = tuple((p.astype(jnp.float32) for p in (w_qkv, bias_qv, w_out, bias_out, gain_attn, shift_attn, w_up, bias_up, w_down, bias_down, gain_ffn, shift_ffn)))
    group = math.gcd(SEQS, max(1, 4096 // SEQ))
    groups = SEQS // group
    x_groups = tokens.reshape(groups, group * SEQ, D)
    cot_groups = cotangent.reshape(groups, group * SEQ, D)
    start_groups = span_start.reshape(groups, group, SPANS)
    len_groups = span_len.reshape(groups, group, SPANS)

    def step(totals, item):
        x_blk, cot_blk, start_blk, len_blk = item
        x_rows = x_blk.astype(jnp.float32)
        layer_out, pull = jax.vjp(forward, x_rows, params)
        grad_y = cot_blk.astype(jnp.float32) * span_mask(start_blk, len_blk)[:, None]
        grad_x, grad_params = pull(grad_y)
        totals = jax.tree.map(lambda a, b: a + b, totals, grad_params)
        return (totals, (layer_out.astype(jnp.bfloat16), grad_x.astype(jnp.bfloat16)))
    zeros = jax.tree.map(jnp.zeros_like, params)
    totals, (outs_all, grads_all) = lax.scan(step, zeros, (x_groups, cot_groups, start_groups, len_groups))
    return (outs_all.reshape(TOKENS, D), grads_all.reshape(TOKENS, D), totals[0], totals[1], totals[2], totals[3], totals[4], totals[5], totals[6], totals[7], totals[8], totals[9], totals[10], totals[11])
```

```python
import jax
import jax.numpy as jnp
from jax import lax
from jax.experimental import pallas as pl
from jax.experimental.pallas import tpu as pltpu
from jax.sharding import PartitionSpec as P

HEAD = 64
SEQ = 512
NORM_EPSILON = 1e-12
F32 = jnp.float32
BF16 = jnp.bfloat16


def span_mask(starts, lengths_in):
    positions = jnp.arange(SEQ, dtype=jnp.int32)
    inside = (positions[None, None, :] >= starts[:, :, None]) & (
        positions[None, None, :] < (starts + lengths_in)[:, :, None]
    )
    return jnp.any(inside, axis=1).astype(F32)


def dot(a, b, dims):
    return lax.dot_general(a, b, (dims, ((), ())), preferred_element_type=F32)


def dot_nn(a, b):
    return dot(a, b, ((1,), (0,)))


def dot_nt(a, b):
    return dot(a, b, ((1,), (1,)))


def dot_tn(a, b):
    return dot(a, b, ((0,), (0,)))


C0 = 0.7978845608028654
C1 = 0.044715
EXP_SCALE = HEAD ** (-0.5) * 1.4426950408889634


def call(body, grid, in_specs, out_specs, out_shape, args, scratch=(), flops=0, transcendentals=0):
    moved = sum(a.size * a.dtype.itemsize for a in args) + sum(o.size * o.dtype.itemsize for o in jax.tree.leaves(out_shape))
    return pl.pallas_call(
        body,
        grid=grid,
        in_specs=in_specs,
        out_specs=out_specs,
        out_shape=out_shape,
        scratch_shapes=list(scratch),
        compiler_params=pltpu.CompilerParams(
            dimension_semantics=("arbitrary",) * len(grid), vmem_limit_bytes=56 * 2**20
        ),
        cost_estimate=pl.CostEstimate(flops=flops, bytes_accessed=moved, transcendentals=transcendentals),
    )(*args)


def shape(dims, dtype):
    return jax.ShapeDtypeStruct(dims, dtype)


def rows_spec(rows, cols):
    return pl.BlockSpec((rows, cols), lambda i: (i, 0))


def whole_spec(a):
    zeros = (0,) * a.ndim
    return pl.BlockSpec(a.shape, lambda *_: zeros, pipeline_mode=pl.Buffered(1))


def fixed_out(dims):
    zeros = (0,) * len(dims)
    return pl.BlockSpec(dims, lambda *_: zeros)


def attend_fwd_body(x_ref, w_ref, b_ref, qkv_ref, ctx_ref, lse_ref):
    w = jnp.concatenate([w_ref[0], w_ref[1], w_ref[2]], axis=1)
    b = jnp.concatenate([b_ref[0], b_ref[1], b_ref[2]], axis=1)
    qkv = (dot_nn(x_ref[...], w) + b).astype(BF16)
    qkv_ref[...] = qkv
    pair = 2 * HEAD
    q, k, v = qkv[:, :pair], qkv[:, pair : 2 * pair], qkv[:, 2 * pair :]
    lane = lax.broadcasted_iota(jnp.int32, (1, pair), 1)
    v_t = v.astype(F32).T.astype(BF16)
    outs, logs = [], []
    for h in range(2):
        mask = ((lane >= h * HEAD) & (lane < (h + 1) * HEAD)).astype(BF16)
        s = dot_nt(k, q * mask)
        top = jnp.max(s, 0, keepdims=True)
        e = jnp.exp2((s - top) * EXP_SCALE)
        total = jnp.sum(e, 0, keepdims=True)
        out = dot_nn(v_t[h * HEAD : (h + 1) * HEAD], e.astype(BF16))
        outs.append(out * (1.0 / total))
        logs.append(top * EXP_SCALE + jnp.log2(total))
    ctx_ref[...] = jnp.concatenate(outs, 0).T.astype(BF16)
    lse_ref[0] = jnp.concatenate(logs + [jnp.zeros((6, SEQ), F32)], 0)


def attend_fwd(x, w, b):
    rows, d = x.shape
    seqs = rows // SEQ
    cols = w.shape[2]
    pair = 2 * HEAD
    pairs = cols // pair
    return call(
        attend_fwd_body,
        (seqs, pairs),
        [
            pl.BlockSpec((SEQ, d), lambda s, p: (s, 0)),
            pl.BlockSpec((3, d, pair), lambda s, p: (0, 0, p)),
            pl.BlockSpec((3, 1, pair), lambda s, p: (0, 0, p)),
        ],
        [
            pl.BlockSpec((SEQ, 3 * pair), lambda s, p: (s, p)),
            pl.BlockSpec((SEQ, pair), lambda s, p: (s, p)),
            pl.BlockSpec((1, 8, SEQ), lambda s, p: (s * pairs + p, 0, 0)),
        ],
        [
            shape((rows, 3 * cols), BF16),
            shape((rows, cols), BF16),
            shape((seqs * pairs, 8, SEQ), F32),
        ],
        (x, w, b),
        flops=2 * rows * d * 3 * cols + 4 * rows * SEQ * cols * 4,
    )


def layer_norm(values):
    mean = jnp.mean(values, -1, keepdims=True)
    centered = values - mean
    factor = lax.rsqrt(jnp.mean(centered * centered, -1, keepdims=True) + NORM_EPSILON)
    return centered * factor, factor


def layer_norm_back(grad, normed, factor, gain):
    scaled = grad * gain
    return factor * (
        scaled
        - jnp.mean(scaled, -1, keepdims=True)
        - normed * jnp.mean(scaled * normed, -1, keepdims=True)
    )


FF_STEP = 512


def ffn_half(low, w_up_ref, b_ref, w_down_ref, act_ref, slope_ref):
    total = None
    for begin in range(0, w_up_ref.shape[1], FF_STEP):
        cols = slice(begin, begin + FF_STEP)
        u = dot_nn(low, w_up_ref[:, cols]) + b_ref[:, cols]
        sq = u * u
        t = jnp.tanh(u * (C0 + (C0 * C1) * sq))
        half = 0.5 + 0.5 * t
        act = (u * half).astype(BF16)
        act_ref[:, cols] = act
        slope_ref[:, cols] = (half + (half - half * half) * u * (2 * C0 + (6 * C0 * C1) * sq)).astype(slope_ref.dtype)
        part = dot_nn(act, w_down_ref[cols, :])
        total = part if total is None else total + part
    return total


def ffn_first_body(c0_ref, c1_ref, x_ref, wo0_ref, wo1_ref, vec_ref, wu_ref, bu_ref, wd_ref,
                   normed_ref, factor_ref, low_ref, act_ref, slope_ref, part_ref):
    attention = dot_nn(c0_ref[...], wo0_ref[...]) + dot_nn(c1_ref[...], wo1_ref[...]) + vec_ref[0:1]
    normed, factor = layer_norm(x_ref[...].astype(F32) + attention)
    normed_ref[...] = normed
    factor_ref[...] = jnp.broadcast_to(factor, factor_ref.shape)
    hidden = normed * vec_ref[1:2] + vec_ref[2:3]
    low = hidden.astype(BF16)
    low_ref[...] = low
    part_ref[...] = hidden + vec_ref[3:4] + ffn_half(low, wu_ref, bu_ref, wd_ref, act_ref, slope_ref)


def ffn_first(c0, c1, x, wo0, wo1, vec, wu, bu, wd):
    rows, d = x.shape
    ff = wu.shape[1]
    r = 256
    return call(
        ffn_first_body,
        (rows // r,),
        [rows_spec(r, c0.shape[1]), rows_spec(r, c1.shape[1]), rows_spec(r, d)]
        + [whole_spec(a) for a in (wo0, wo1, vec, wu, bu, wd)],
        [rows_spec(r, d), rows_spec(r, 128), rows_spec(r, d), rows_spec(r, ff), rows_spec(r, ff), rows_spec(r, d)],
        [shape((rows, d), F32), shape((rows, 128), F32), shape((rows, d), BF16),
         shape((rows, ff), BF16), shape((rows, ff), BF16), shape((rows, d), F32)],
        (c0, c1, x, wo0, wo1, vec, wu, bu, wd),
        flops=2 * rows * d * d + 4 * rows * d * ff,
    )


def ffn_second_body(low_ref, part_ref, cot_ref, mask_ref, vec_ref, wu_ref, bu_ref, wd_ref,
                    act_ref, slope_ref, out_ref, gr_ref, gfo_ref, sums_ref):
    resid = part_ref[...] + ffn_half(low_ref[...], wu_ref, bu_ref, wd_ref, act_ref, slope_ref)
    normed, factor = layer_norm(resid)
    out_ref[...] = (normed * vec_ref[4:5] + vec_ref[5:6]).astype(BF16)
    grad_y = cot_ref[...].astype(F32) * mask_ref[:, 0:1]
    grad = layer_norm_back(grad_y, normed, factor, vec_ref[4:5])
    gr_ref[...] = grad
    low = grad.astype(BF16)
    gfo_ref[...] = low

    @pl.when(pl.program_id(0) == 0)
    def _():
        sums_ref[...] = jnp.zeros_like(sums_ref)

    sums_ref[0:1] += jnp.sum(low.astype(F32), 0, keepdims=True)
    sums_ref[1:2] += jnp.sum(grad_y * normed, 0, keepdims=True)
    sums_ref[2:3] += jnp.sum(grad_y, 0, keepdims=True)


def ffn_second(low, part, cot, mask, vec, wu, bu, wd):
    rows, d = low.shape
    ff = wu.shape[1]
    r = 256
    return call(
        ffn_second_body,
        (rows // r,),
        [rows_spec(r, d), rows_spec(r, d), rows_spec(r, d), rows_spec(r, mask.shape[1])]
        + [whole_spec(a) for a in (vec, wu, bu, wd)],
        [rows_spec(r, ff), rows_spec(r, ff), rows_spec(r, d), rows_spec(r, d), rows_spec(r, d), fixed_out((8, d))],
        [shape((rows, ff), BF16), shape((rows, ff), BF16), shape((rows, d), BF16), shape((rows, d), F32),
         shape((rows, d), BF16), shape((8, d), F32)],
        (low, part, cot, mask, vec, wu, bu, wd),
        flops=4 * rows * d * ff,
    )


def ffn_back_body(gfo_ref, gr_ref, s0_ref, s1_ref, normed_ref, factor_ref, vec_ref,
                  wu0_ref, wu1_ref, wd0_ref, wd1_ref, wo0_ref, wo1_ref,
                  gp0_ref, gp1_ref, ga_ref, gra_ref, dc0_ref, dc1_ref, bu0_ref, bu1_ref, sums_ref):
    @pl.when(pl.program_id(0) == 0)
    def _():
        sums_ref[...] = jnp.zeros_like(sums_ref)
        bu0_ref[...] = jnp.zeros_like(bu0_ref)
        bu1_ref[...] = jnp.zeros_like(bu1_ref)

    gfo = gfo_ref[...]
    total = gr_ref[...]
    for wu_ref, wd_ref, s_ref, gp_ref, bu_ref in (
        (wu0_ref, wd0_ref, s0_ref, gp0_ref, bu0_ref),
        (wu1_ref, wd1_ref, s1_ref, gp1_ref, bu1_ref),
    ):
        for begin in range(0, wu_ref.shape[1], FF_STEP):
            cols = slice(begin, begin + FF_STEP)
            g = dot_nt(gfo, wd_ref[cols, :]) * s_ref[:, cols].astype(F32)
            low = g.astype(BF16)
            gp_ref[:, cols] = low
            bu_ref[0:1, cols] += jnp.sum(low.astype(F32), 0, keepdims=True)
            total = total + dot_nt(low, wu_ref[:, cols])
    normed = normed_ref[...]
    grad = layer_norm_back(total, normed, factor_ref[:, 0:1], vec_ref[1:2])
    gra_ref[...] = grad
    low = grad.astype(BF16)
    ga_ref[...] = low
    dc0_ref[...] = dot_nt(low, wo0_ref[...]).astype(BF16)
    dc1_ref[...] = dot_nt(low, wo1_ref[...]).astype(BF16)
    sums_ref[0:1] += jnp.sum(low.astype(F32), 0, keepdims=True)
    sums_ref[1:2] += jnp.sum(total * normed, 0, keepdims=True)
    sums_ref[2:3] += jnp.sum(total, 0, keepdims=True)


def ffn_back(gfo, gr, s0, s1, normed, factor, vec, wu, wd, wo):
    rows, d = gfo.shape
    ff = wu[0].shape[1]
    hc = wo[0].shape[0]
    r = 256
    return call(
        ffn_back_body,
        (rows // r,),
        [rows_spec(r, d), rows_spec(r, d), rows_spec(r, ff), rows_spec(r, ff), rows_spec(r, d), rows_spec(r, 128)]
        + [whole_spec(a) for a in (vec, *wu, *wd, *wo)],
        [rows_spec(r, ff), rows_spec(r, ff), rows_spec(r, d), rows_spec(r, d), rows_spec(r, hc), rows_spec(r, hc),
         fixed_out((8, ff)), fixed_out((8, ff)), fixed_out((8, d))],
        [shape((rows, ff), BF16), shape((rows, ff), BF16), shape((rows, d), BF16), shape((rows, d), F32),
         shape((rows, hc), BF16), shape((rows, hc), BF16), shape((8, ff), F32), shape((8, ff), F32),
         shape((8, d), F32)],
        (gfo, gr, s0, s1, normed, factor, vec, *wu, *wd, *wo),
        flops=8 * rows * d * ff + 2 * rows * d * d,
    )


def attend_back_body(qkv_ref, ctx_ref, lse_ref, dc_ref, x_ref, w_ref, gi_ref, gx_ref, gw_ref, gb_ref, acc_ref, bacc_ref):
    seq, p = pl.program_id(0), pl.program_id(1)
    pair = 2 * HEAD
    q, k, v = qkv_ref[:, :pair], qkv_ref[:, pair : 2 * pair], qkv_ref[:, 2 * pair :]
    g = dc_ref[...]
    lane = lax.broadcasted_iota(jnp.int32, (1, pair), 1)
    k_t = k.astype(F32).T.astype(BF16)
    delta = (g.astype(F32) * ctx_ref[...].astype(F32)).T
    gq_t = []
    gk = gv = None
    for h in range(2):
        hs = slice(h * HEAD, (h + 1) * HEAD)
        mask = ((lane >= h * HEAD) & (lane < (h + 1) * HEAD)).astype(BF16)
        qm, gm = q * mask, g * mask
        s = dot_nt(k, qm)
        probs = jnp.exp2(s * EXP_SCALE - lse_ref[0, h : h + 1])
        dp = dot_nt(v, gm)
        ds = (probs * (dp - jnp.sum(delta[hs], 0, keepdims=True))).astype(BF16)
        gv_h = dot_nn(probs.astype(BF16), gm)
        gk_h = dot_nn(ds, qm)
        gv = gv_h if gv is None else gv + gv_h
        gk = gk_h if gk is None else gk + gk_h
        gq_t.append(dot_nn(k_t[hs], ds))
    scale = HEAD ** (-0.5)
    gq = (jnp.concatenate(gq_t, 0).T * scale).astype(BF16)
    grads = jnp.concatenate([gq, (gk * scale).astype(BF16), gv.astype(BF16)], 1)
    w = jnp.concatenate([w_ref[0], w_ref[1], w_ref[2]], axis=1)
    part = dot_nt(grads, w)

    @pl.when(p == 0)
    def _():
        gx_ref[...] = gi_ref[...] + part

    @pl.when(p > 0)
    def _():
        gx_ref[...] += part

    gw = dot_tn(x_ref[...], grads)
    gb = jnp.sum(grads.astype(F32), 0, keepdims=True)

    @pl.when(seq == 0)
    def _():
        acc_ref[p] = gw
        bacc_ref[p, 0:1] = gb

    @pl.when(seq > 0)
    def _():
        acc_ref[p] += gw
        bacc_ref[p, 0:1] += gb

    total = acc_ref[p]
    tb = bacc_ref[p, 0:1]
    for c in range(3):
        gw_ref[c] = total[:, c * pair : (c + 1) * pair].astype(BF16)
        gb_ref[c] = tb[:, c * pair : (c + 1) * pair]


def attend_back(qkv, ctx, lse, dc, x, w, gi):
    rows, d = x.shape
    seqs = rows // SEQ
    cols = w.shape[2]
    pair = 2 * HEAD
    pairs = cols // pair
    last = seqs - 1
    return call(
        attend_back_body,
        (seqs, pairs),
        [
            pl.BlockSpec((SEQ, 3 * pair), lambda s, p: (s, p)),
            pl.BlockSpec((SEQ, pair), lambda s, p: (s, p)),
            pl.BlockSpec((1, 8, SEQ), lambda s, p: (s * pairs + p, 0, 0)),
            pl.BlockSpec((SEQ, pair), lambda s, p: (s, p)),
            pl.BlockSpec((SEQ, d), lambda s, p: (s, 0)),
            pl.BlockSpec((3, d, pair), lambda s, p: (0, 0, p)),
            pl.BlockSpec((SEQ, d), lambda s, p: (s, 0)),
        ],
        [
            pl.BlockSpec((SEQ, d), lambda s, p: (s, 0)),
            pl.BlockSpec((3, d, pair), lambda s, p: (0, 0, jnp.where(s == last, p, 0))),
            pl.BlockSpec((3, 1, pair), lambda s, p: (0, 0, jnp.where(s == last, p, 0))),
        ],
        [shape((rows, d), F32), shape((3, d, cols), BF16), shape((3, 1, cols), F32)],
        (qkv, ctx, lse, dc, x, w, gi),
        scratch=[pltpu.VMEM((pairs, d, 3 * pair), F32), pltpu.VMEM((pairs, 8, 3 * pair), F32)],
        flops=4 * rows * d * 3 * cols + 10 * rows * SEQ * cols * 4,
    )


def grad_tn_body(a_ref, b_ref, o_ref):
    o_ref[...] = dot_tn(a_ref[...], b_ref[...]).astype(o_ref.dtype)


def grad_tn(a, b, block):
    rows, m = a.shape
    n = b.shape[1]
    return call(
        grad_tn_body,
        (m // block,),
        [pl.BlockSpec((rows, block), lambda i: (0, i)), whole_spec(b)],
        pl.BlockSpec((block, n), lambda i: (i, 0)),
        shape((m, n), BF16),
        (a, b),
        flops=2 * rows * m * n,
    )


def grad_tn_cols(a, b, block):
    rows, m = a.shape
    n = b.shape[1]
    return call(
        grad_tn_body,
        (n // block,),
        [whole_spec(a), pl.BlockSpec((rows, block), lambda i: (0, i))],
        pl.BlockSpec((m, block), lambda i: (0, i)),
        shape((m, n), BF16),
        (a, b),
        flops=2 * rows * m * n,
    )


class Links:
    def __init__(self):
        self.size = lax.axis_size("dp")
        self.index = lax.axis_index("dp")
        self.far = self.size // 4

    def across(self, value):
        return lax.ppermute(value, "tensor", [(0, 1), (1, 0)])

    def swap(self, value, bits):
        return lax.ppermute(value, "dp", [(i, i ^ bits) for i in range(self.size)])

    def other_half(self, own, axis):
        part = own.shape[axis] // 4
        quarter = self.index & 3
        first = self.across(lax.dynamic_slice_in_dim(own, quarter * part, part, axis))
        second = self.swap(first, 2)
        third = self.swap(first, 1)
        fourth = self.swap(second, 1)
        whole = jnp.zeros_like(own)
        for order, piece in ((0, first), (2, second), (1, third), (3, fourth)):
            whole = lax.dynamic_update_slice_in_dim(whole, piece, (quarter ^ order) * part, axis)
        return whole

    def reduce(self, own, other, axis):
        half = own.shape[axis] // 2
        core = self.index & 1
        row = (self.index >> 1) & 1
        far = self.index >> 2

        def take(value, position, length):
            return lax.dynamic_slice_in_dim(value, position * length, length, axis)

        def add(a, *rest):
            total = a.astype(F32)
            for value in rest:
                total = total + value.astype(F32)
            return total

        other_sum = add(take(other, core, half), self.swap(take(other, 1 - core, half), 1)).astype(BF16)
        own_sum = add(
            take(own, core, half),
            self.swap(take(own, 1 - core, half), 1),
            self.across(other_sum),
        ).astype(BF16)
        quarter = half // 2
        quarter_sum = add(take(own_sum, row, quarter), self.swap(take(own_sum, 1 - row, quarter), 2)).astype(BF16)
        piece = quarter // self.far
        parts = [take(quarter_sum, far, piece)]
        for step in range(1, self.far):
            parts.append(self.swap(take(quarter_sum, far ^ step, piece), 4 * step))
        total = add(*parts).astype(BF16)
        def put(whole, value, position):
            return lax.dynamic_update_slice_in_dim(whole, value, position * value.shape[axis], axis)

        shape = list(own.shape)
        shape[axis] = quarter
        spread = put(jnp.zeros(shape, BF16), total, far)
        for step in range(1, self.far):
            spread = put(spread, self.swap(total, 4 * step), far ^ step)
        shape[axis] = half
        wide = put(put(jnp.zeros(shape, BF16), spread, row), self.swap(spread, 2), 1 - row)
        final = put(put(jnp.zeros(own.shape, BF16), wide, core), self.swap(wide, 1), 1 - core)
        return final.astype(F32)

    def reduce_small(self, own, other, shared):
        got_other = self.across(other)
        got_shared = self.across(shared)
        total = jnp.concatenate([own + got_other, shared + got_shared])
        bits = 1
        while bits < self.size:
            total = total + self.swap(total, bits)
            bits *= 2
        return total[: own.shape[0]], total[own.shape[0] :]


def local(
    tokens,
    w_qkv,
    bias_qv,
    w_out,
    bias_out,
    gain_attn,
    shift_attn,
    w_up,
    bias_up,
    w_down,
    bias_down,
    gain_ffn,
    shift_ffn,
    cotangent,
    span_start,
    span_len,
):
    links = Links()
    own_seqs = tokens.shape[0] // SEQ
    mask_group = span_mask(span_start, span_len)
    mask_own = lax.dynamic_slice_in_dim(
        mask_group, lax.axis_index("tensor") * own_seqs, own_seqs, 0
    )
    bias_out, gain_attn, shift_attn, bias_down, gain_ffn, shift_ffn = [
        p.astype(F32) for p in (bias_out, gain_attn, shift_attn, bias_down, gain_ffn, shift_ffn)
    ]
    w_qkv2 = (w_qkv, links.other_half(w_qkv, 1))
    w_out2 = (w_out, links.other_half(w_out, 0))
    w_up2 = (w_up, links.other_half(w_up, 0))
    w_down2 = (w_down, links.other_half(w_down, 0))
    bias_qv2 = (bias_qv, links.across(bias_qv))
    bias_up2 = (bias_up, links.across(bias_up))
    head_cols = w_qkv.shape[2]
    d = tokens.shape[1]
    vec = jnp.stack([bias_out, gain_attn, shift_attn, bias_down, gain_ffn, shift_ffn] + [bias_out] * 2)
    mask_rows = jnp.broadcast_to(mask_own.reshape(-1)[:, None], (tokens.shape[0], 128))
    bias3 = [
        jnp.stack([b[0], jnp.zeros_like(b[0]), b[1]]).astype(F32).reshape(3, 1, head_cols) for b in bias_qv2
    ]
    bias_up2 = [b.astype(F32).reshape(1, -1) for b in bias_up2]

    saved = [attend_fwd(tokens, w_qkv2[side], bias3[side]) for side in range(2)]
    normed, factor, low, act0, slope0, part = ffn_first(
        saved[0][1], saved[1][1], tokens, *w_out2, vec, w_up2[0], bias_up2[0], w_down2[0]
    )
    act1, slope1, layer_out, grad_resid_ffn, grad_ffn_out, ffn_sums = ffn_second(
        low, part, cotangent, mask_rows, vec, w_up2[1], bias_up2[1], w_down2[1]
    )
    grad_bias_down, grad_gain_ffn, grad_shift_ffn = ffn_sums[0], ffn_sums[1], ffn_sums[2]
    grad_down2 = [grad_tn(a, grad_ffn_out, 512) for a in (act0, act1)]
    grad_down = links.reduce(*grad_down2, 0)
    gp0, gp1, grad_attn, grad_resid_attn, dc0, dc1, bu0, bu1, attn_sums = ffn_back(
        grad_ffn_out, grad_resid_ffn, slope0, slope1, normed, factor, vec, w_up2, w_down2, w_out2
    )
    grad_bias_out, grad_gain_attn, grad_shift_attn = attn_sums[0], attn_sums[1], attn_sums[2]
    grad_bias_up2 = [bu0[0], bu1[0]]
    grad_up = links.reduce(*[grad_tn_cols(low, g, 512) for g in (gp0, gp1)], 0)
    grad_out = links.reduce(*[grad_tn(saved[side][1], grad_attn, 384) for side in range(2)], 0)
    grad_tokens = grad_resid_attn
    grad_qkv2, grad_bias_qv2 = [None, None], [None, None]
    for side in (1, 0):
        qkv, ctx, lse = saved[side]
        grad_tokens, grad_qkv2[side], gb = attend_back(
            qkv, ctx, lse, (dc0, dc1)[side], tokens, w_qkv2[side], grad_tokens
        )
        grad_bias_qv2[side] = jnp.concatenate([gb[0, 0], gb[2, 0]])
    grad_qkv = links.reduce(*grad_qkv2, 1)
    own_small, shared_small = links.reduce_small(
        jnp.concatenate([grad_bias_qv2[0], grad_bias_up2[0]]),
        jnp.concatenate([grad_bias_qv2[1], grad_bias_up2[1]]),
        jnp.concatenate(
            [grad_bias_out, grad_gain_attn, grad_shift_attn, grad_bias_down, grad_gain_ffn, grad_shift_ffn]
        ),
    )
    shared = shared_small.reshape(6, -1)
    return (
        layer_out,
        grad_tokens.astype(BF16),
        grad_qkv,
        own_small[: 2 * head_cols].reshape(2, head_cols),
        grad_out,
        shared[0],
        shared[1],
        shared[2],
        grad_up,
        own_small[2 * head_cols :],
        grad_down,
        shared[3],
        shared[4],
        shared[5],
    )


def solution(mesh):
    in_specs = (
        P(("dp", "tensor"), None),
        P(None, None, "tensor"),
        P(None, "tensor"),
        P("tensor", None),
        P(),
        P(),
        P(),
        P(None, "tensor"),
        P("tensor"),
        P("tensor", None),
        P(),
        P(),
        P(),
        P(("dp", "tensor"), None),
        P("dp", None),
        P("dp", None),
    )
    out_specs = (
        P(("dp", "tensor"), None),
        P(("dp", "tensor"), None),
        P(None, None, "tensor"),
        P(None, "tensor"),
        P("tensor", None),
        P(),
        P(),
        P(),
        P(None, "tensor"),
        P("tensor"),
        P("tensor", None),
        P(),
        P(),
        P(),
    )
    return jax.shard_map(local, mesh=mesh, in_specs=in_specs, out_specs=out_specs, check_vma=False)
```
